1024 devices in a mesh: gz: 16 (over z_lo), gy: 8 (over y, z_hi), gx: 8 (over x, core).
Axes of the slice: x: 4, y: 4, z: 32 (z_hi: 2, z_lo: 16; z = z_hi * 16 + z_lo), core: 2. Of those that a mesh axis runs over, the one named last changes fastest.
Arguments:
- positions: float32 [3, 48, 24, 24, 128], P(None, 'gz', 'gy', 'gx'), may hold values from 0 to 1
- velocities: float32 [3, 48, 24, 24, 128], P(None, 'gz', 'gy', 'gx'), may hold values from -6 to 6
- counts: int32 [48, 24, 24], P('gz', 'gy', 'gx'), may hold values from 64 to 128
- bonds: int32 [2, 48, 24, 24, 128], P(None, 'gz', 'gy', 'gx'), may hold values from 0 to 127
- plan_z: int32 [16], replicated, may hold values from 0 to 2
- plan_y: int32 [16, 8], replicated, may hold values from 0 to 2
- plan_x: int32 [16, 8, 8], replicated, may hold values from 0 to 2
Outputs:
- forces_first: float32 [3, 48, 24, 24, 128], P(None, 'gz', 'gy', 'gx')
- moved_positions: float32 [3, 80, 40, 40, 128], P(None, 'gz', 'gy', 'gx')
- moved_forces: float32 [3, 80, 40, 40, 128], P(None, 'gz', 'gy', 'gx')
The draws below stay inside these ranges and needn't reach their ends.
Inputs may be any that keep to these rules, and one draw needn't show every extreme that they name: `counts`: bead b of a cell is present when b is less than the cell's count. `bonds`: both ends of a bond are bead places of the bond's own cell; a bond counts only when both ends are present. `plan_z`: entry i is the number of cells by which the boundary between brick planes i and i + 1 (the last with plane 0) moves up. `plan_y`: entry (i, j) is the number of cells by which the boundary between columns j and j + 1 of plane i (the last with column 0) moves up. `plan_x`: entry (i, j, k) is the number of cells by which the boundary between bricks k and k + 1 of column (i, j) (the last with brick 0) moves up.
All inputs are finite; a program needn't handle non-finite values.
Results may differ from the reference program's by a relative error of at most 0.0001.
Values sent between devices are 32-bit elements; how exact they have to be, the bound alone decides.
No kernel may reach another device: no remote copies, remote signals or barrier semaphores. Data moves between devices by JAX's collectives and lax.ppermute only.
A program may use at most 32 MiB of HBM per device.

```python
import jax
import jax.numpy as jnp
from jax import lax

CELLS = 3
BEADS = 128
BONDS = 128
SLOTS = 5
NZ = 48
NY = 24
NX = 24
MZ = 80
MY = 40
MX = 40
N_GZ = 16
N_GY = 8
N_GX = 8


def plant(entries, stream_key, least, largest):
    place = [jax.random.randint(jax.random.fold_in(stream_key, axis), (), 0, length) for axis, length in enumerate(entries.shape)]
    widest = entries.shape.index(max(entries.shape))
    neighbour = place[:widest] + [(place[widest] + 1) % entries.shape[widest]] + place[widest + 1:]
    return entries.at[tuple(place)].set(least).at[tuple(neighbour)].set(largest)


def block_scale(key, shape, shards, least, high):
    def one(dim, parts):
        heights = jax.random.uniform(jax.random.fold_in(jax.random.fold_in(key, 6), dim), (parts,), jnp.float32, least / len(shards), high / len(shards))
        return jnp.repeat(jnp.exp(heights), shape[dim] // parts).reshape((-1,) + (1,) * (len(shape) - dim - 1))

    factor_of = one(*shards[0])
    for cut in shards[1:]:
        factor_of = factor_of * one(*cut)
    return factor_of


def scatter_about(own_key, shape, scale, most, shards=(), kind=jnp.bfloat16):
    values = jax.random.normal(own_key, shape, jnp.float32) * scale
    if len(shards) > 0:
        values = block_scale(own_key, shape, shards, -0.22, 0.18) * values
    return jnp.clip(values, min=-most, max=most).astype(kind)


def setup_inputs(seed: int = 0) -> dict:
    keys = jax.random.split(jax.random.key(seed), 8)
    return {
        "positions": jnp.clip(1.0 * jax.random.uniform(keys[0], (3, NZ, NY, NX, BEADS), jnp.float32) ** block_scale(keys[0], (3, NZ, NY, NX, BEADS), ((1, 16), (2, 8), (3, 8)), -0.2, 0.2), 0.0, 1.0),
        "velocities": scatter_about(keys[1], (3, NZ, NY, NX, BEADS), 1.0, 6.0, ((1, 16), (2, 8), (3, 8)), jnp.float32),
        "counts": plant(jax.random.randint(keys[2], (NZ, NY, NX), BEADS // 2, BEADS + 1), jax.random.fold_in(keys[2], 1), BEADS // 2, BEADS).astype(jnp.int32),
        "bonds": plant(jax.random.randint(keys[3], (2, NZ, NY, NX, BONDS), 0, BEADS), jax.random.fold_in(keys[3], 1), 0, BEADS - 1).astype(jnp.int32),
        "plan_z": plant(jax.random.randint(keys[4], (N_GZ,), 0, 3), jax.random.fold_in(keys[4], 1), 0, 2).astype(jnp.int32),
        "plan_y": plant(jax.random.randint(keys[5], (N_GZ, N_GY), 0, 3), jax.random.fold_in(keys[5], 1), 0, 2).astype(jnp.int32),
        "plan_x": plant(jax.random.randint(keys[6], (N_GZ, N_GY, N_GX), 0, 3), jax.random.fold_in(keys[6], 1), 0, 2).astype(jnp.int32),
    }


STRENGTH = 0.3
SPREAD = 0.6
BOND_STIFF = 1.0
STEP_DT = 0.2
ALL_OFFSETS = [(along_z, along_y, along_x) for along_z in (-1, 0, 1) for along_y in (-1, 0, 1) for along_x in (-1, 0, 1)]


def pair_block(own_beads, own_alive, partner, partner_alive, offset):
    offset_vec = jnp.array(offset, dtype=jnp.float32).reshape(3, 1, 1, 1)
    separation = own_beads[:, :, :, None] - partner[:, :, None, :] - offset_vec
    distance = jnp.sum(separation * separation, axis=0)
    weight = STRENGTH * jnp.exp(-distance / SPREAD) * own_alive[:, :, None] * partner_alive[:, None, :]
    return jnp.sum(weight[None] * separation, axis=3)


def pair_forces(coords, living):
    padded = jnp.concatenate([coords[:, -1:], coords, coords[:, :1]], axis=1)
    padded_live = jnp.concatenate([living[-1:], living, living[:1]], axis=0)

    def plane_forces(plane_index):
        three_planes = lax.dynamic_slice_in_dim(padded, plane_index, 3, 1)
        three_live = lax.dynamic_slice_in_dim(padded_live, plane_index, 3, 0)
        own_beads = three_planes[:, 1].reshape(3, -1, BEADS)
        own_alive = three_live[1].reshape(-1, BEADS)
        summed = jnp.zeros_like(own_beads)
        for offset in ALL_OFFSETS:
            partner = jnp.roll(three_planes[:, 1 + offset[0]], (-offset[1], -offset[2]), axis=(1, 2)).reshape(3, -1, BEADS)
            partner_alive = jnp.roll(three_live[1 + offset[0]], (-offset[1], -offset[2]), axis=(0, 1)).reshape(-1, BEADS)
            summed = summed + pair_block(own_beads, own_alive, partner, partner_alive, offset)
        return summed.reshape(3, NY, NX, BEADS)

    planes = lax.map(plane_forces, jnp.arange(NZ, dtype=jnp.int32))
    return jnp.moveaxis(planes, 0, 1)


def bond_forces(coords, living, bonds):
    flat_coords = coords.reshape(3, -1, BEADS)
    flat_alive = living.reshape(-1, BEADS)
    head_ends = bonds[0].reshape(-1, BONDS)
    tail_ends = bonds[1].reshape(-1, BONDS)
    head_wide = jnp.broadcast_to(head_ends[None], (3,) + head_ends.shape)
    tail_wide = jnp.broadcast_to(tail_ends[None], (3,) + tail_ends.shape)
    head_pos = jnp.take_along_axis(flat_coords, head_wide, axis=2)
    tail_pos = jnp.take_along_axis(flat_coords, tail_wide, axis=2)
    bonded = jnp.take_along_axis(flat_alive, head_ends, axis=1) * jnp.take_along_axis(flat_alive, tail_ends, axis=1)
    tension = BOND_STIFF * bonded[None] * (tail_pos - head_pos)
    cell_ids = jnp.arange(flat_coords.shape[1], dtype=jnp.int32)[:, None]
    summed = jnp.zeros_like(flat_coords)
    summed = summed.at[:, cell_ids, head_ends].add(tension)
    summed = summed.at[:, cell_ids, tail_ends].add(-tension)
    return summed.reshape(coords.shape)


def all_forces(coords, living, bonds):
    return pair_forces(coords, living) + bond_forces(coords, living, bonds)


def placement(plan_table, extent):
    owner_count = plan_table.shape[-1]
    lowered = jnp.roll(plan_table, 1, axis=-1)
    filled = CELLS + plan_table - lowered
    owners = jnp.arange(owner_count, dtype=jnp.int32)
    slot_index = jnp.arange(SLOTS, dtype=jnp.int32)
    first_cell = owners * CELLS + lowered
    target = (first_cell[..., None] + slot_index) % extent
    usable = slot_index < filled[..., None]
    grid_index = jnp.arange(extent, dtype=jnp.int32)
    matches = (target[..., None] == grid_index) & usable[..., None]
    return matches.astype(jnp.float32)


def relayout(carried, plan_z, plan_y, plan_x):
    components = carried.shape[0]
    along_z = placement(plan_z, NZ)
    step_one = jnp.einsum('htz,czyxb->chtyxb', along_z, carried, precision=lax.Precision.HIGHEST)
    along_y = placement(plan_y, NY)
    step_two = jnp.einsum('hjty,chsyxb->chsjtxb', along_y, step_one, precision=lax.Precision.HIGHEST)
    along_x = placement(plan_x, NX)
    step_three = jnp.einsum('hjgux,chsjtxb->chsjtgub', along_x, step_two, precision=lax.Precision.HIGHEST)
    return step_three.reshape(components, MZ, MY, MX, BEADS)


def reference(positions, velocities, counts, bonds, plan_z, plan_y, plan_x):
    living = (jnp.arange(BEADS, dtype=jnp.int32) < counts[..., None]).astype(jnp.float32)
    forces_first = all_forces(positions, living, bonds)
    stepped = positions + STEP_DT * velocities + (0.5 * STEP_DT * STEP_DT) * forces_first
    forces_next = all_forces(stepped, living, bonds)
    carried = jnp.concatenate([stepped * living[None], forces_next], axis=0)
    moved = relayout(carried, plan_z, plan_y, plan_x)
    return forces_first, moved[:3], moved[3:]
```

```python
import functools
import math

import jax
import jax.numpy as jnp
from jax import lax
from jax.experimental import pallas as pl
from jax.experimental.pallas import tpu as pltpu
from jax.sharding import PartitionSpec as P

STRENGTH = 0.3
SPREAD = 0.6
STEP_DT = 0.2
F32 = jnp.float32
BF16 = jnp.bfloat16
SCALE = math.sqrt(1.0 / (SPREAD * math.log(2.0)))
PUSH = STRENGTH / SCALE
DEAD = -1.0e6
N = 128
V = pl.BlockSpec(memory_space=pltpu.VMEM)
S = pl.BlockSpec(memory_space=pltpu.SMEM)


def call(kernel, name, ins, outs, scratch=(), specs=None, to_hbm=False):
    specs = [V] * len(ins) if specs is None else specs
    return pl.pallas_call(
        kernel,
        name=name,
        out_shape=[
            (jax.ShapeDtypeStruct if to_hbm else pltpu.VMEM)(shape, F32) for shape in outs
        ],
        in_specs=specs,
        out_specs=[V] * len(outs),
        scratch_shapes=list(scratch),
    )(*[
        pltpu.with_memory_space_constraint(value, pltpu.VMEM) if spec is V else value
        for value, spec in zip(ins, specs)
    ])


def living_row(count):
    return (lax.broadcasted_iota(jnp.int32, (1, N), 1) < count).astype(F32)


def pack_first(pos, counts, own, top, bottom):
    for z in range(3):
        for y in range(3):
            for x in range(3):
                rows = [pos[k, z, y, x : x + 1, :] for k in range(3)]
                cell = jnp.concatenate(rows + [living_row(counts[z, y, x])], axis=0)
                own[9 * z + 3 * y + x] = cell
                if z == 2:
                    top[3 * y + x] = cell
                if z == 0:
                    bottom[3 * y + x] = cell


SWAP_CELLS = [
    (p, y, x)
    for p in range(-1, 4)
    for y in (range(3) if p in (-1, 3) else (0, 2))
    for x in range(3)
]
SWAP_AT = {cell: at for at, cell in enumerate(SWAP_CELLS)}


def pack_swap(own, low, high, out):
    for (p, y, x), at in SWAP_AT.items():
        if p == -1:
            out[at] = low[3 * y + x]
        elif p == 3:
            out[at] = high[3 * y + x]
        else:
            out[at] = own[9 * p + 3 * y + x]


def even_column():
    return lax.axis_index("gy") % 2 == 0


def lowest_plane():
    return lax.axis_index("gz") == 0


def highest_plane():
    return lax.axis_index("gz") == 15


def partner_cell(low, high, swapped, p, y, x):
    there = swapped[SWAP_AT[p, y, x]]
    if p == -1:
        return jnp.where(lowest_plane(), low[3 * y + x], there)
    if p == 3:
        return jnp.where(highest_plane(), high[3 * y + x], there)
    return there


def own_cell(own, low, high, swapped, p, y, x):
    if p == -1:
        return jnp.where(lowest_plane(), swapped[SWAP_AT[p, y, x]], low[3 * y + x])
    if p == 3:
        return jnp.where(highest_plane(), swapped[SWAP_AT[p, y, x]], high[3 * y + x])
    return own[9 * p + 3 * y + x]


def pack_relay(low, high, swapped, out):
    even = even_column()
    for p in range(-1, 4):
        for x in range(3):
            upper = partner_cell(low, high, swapped, p, 2, x)
            lower = partner_cell(low, high, swapped, p, 0, x)
            out[3 * (p + 1) + x] = jnp.where(even, upper, lower)


def pack_middle(own, low, high, swapped, relayed, middle, left, right):
    even = even_column()
    for p in range(-1, 4):
        for y in range(-1, 4):
            for x in range(3):
                if y in (-1, 3):
                    near = partner_cell(low, high, swapped, p, 2 if y == -1 else 0, x)
                    far = relayed[3 * (p + 1) + x]
                    if y == -1:
                        near, far = far, near
                    cell = jnp.where(even, near, far)
                else:
                    cell = own_cell(own, low, high, swapped, p, y, x)
                row = 5 * (p + 1) + y + 1
                middle[3 * row + x] = cell
                if x == 0:
                    left[row] = cell
                if x == 2:
                    right[row] = cell


def three(x):
    first = x.astype(BF16).astype(F32)
    rest = x - first
    second = rest.astype(BF16).astype(F32)
    return first, second, rest - second


def scaled_cell(cell, p, y, x):
    alive = cell[3:4] > 0.5
    at = lax.broadcasted_iota(jnp.int32, (3, 1), 0)
    shift = jnp.where(at == 0, p, jnp.where(at == 1, y, x)).astype(F32) - 1.5
    return jnp.where(alive, (cell[0:3] + shift) * SCALE, 0.0), alive


def partner_rows(coords, alive):
    norm = jnp.where(alive, -jnp.sum(coords * coords, axis=0, keepdims=True), DEAD)
    b1, b2, b3 = three(jnp.concatenate([coords, norm], axis=0))
    ones = jnp.concatenate([jnp.ones((3, N), F32), jnp.zeros((1, N), F32)], axis=0)
    zeros = jnp.zeros((4, N), F32)
    return jnp.concatenate([zeros, b1, b1, b2, b1, b2, b3, ones], axis=0)


def own_rows(coords):
    norm = -jnp.sum(coords * coords, axis=0, keepdims=True)
    a1, a2, a3 = three(jnp.concatenate([2.0 * coords, jnp.ones((1, N), F32)], axis=0))
    zeros = jnp.zeros((1, N), F32)
    tail = jnp.concatenate(list(three(norm)) + [zeros], axis=0)
    return jnp.concatenate([jnp.zeros((4, N), F32), a1, a2, a1, a3, a2, a1, tail], axis=0)


def product(left, right, right_turned=False):
    dims = (((1,), (1 if right_turned else 0,)), ((), ()))
    return lax.dot_general(left, right, dims, preferred_element_type=F32)


def store_operands(rows, at, b_ref, x_ref):
    b_ref[at] = rows.T.astype(BF16)
    x_ref[at] = rows[16:32].astype(BF16)


AHEAD = 8


def push_rows(acc_ref, blocks, b_ref, x_ref, a_ref):
    def reach(block):
        return max(0, block[1] - 1), min(2, block[1] + 1) + 1

    def exponents(block):
        first, last = reach(block)
        return product(b_ref[block[2]], a_ref[block[0], :, N * first : N * last])

    waiting = [exponents(block) for block in blocks[:AHEAD]]
    sums = [None, None, None]
    for at, block in enumerate(blocks):
        if at + AHEAD < len(blocks):
            waiting.append(exponents(blocks[at + AHEAD]))
        weight = jnp.exp2(waiting.pop(0))
        high = weight.astype(BF16)
        low = (weight - high.astype(F32)).astype(BF16)
        x_op = x_ref[block[2]]
        value = product(
            jnp.concatenate([x_op, x_op], axis=1), jnp.concatenate([high, low], axis=0)
        )
        first, last = reach(block)
        for x in range(first, last):
            part = value[:, N * (x - first) : N * (x - first + 1)]
            sums[x] = part if sums[x] is None else sums[x] + part
        if at + 1 == len(blocks) or blocks[at + 1][3] != block[3]:
            for x in range(3):
                if sums[x] is not None:
                    acc_ref[3 * block[0] + x] += sums[x]
            sums = [None, None, None]


def cell_force(acc, coords):
    total = acc[0:4] + acc[4:8] + acc[8:12]
    return PUSH * (coords * acc[12:15] - total[0:3])


def z_pair(step):
    z = (step + 1) // 3
    return z, step - 2 * z


def own_pairs(own, counts, bonds, acc_out, bond_out, b_ref, x_ref, a_ref):
    def prepare(row, _):
        z, y = row // 3, row % 3
        for x in range(3):
            coords, alive = scaled_cell(own[3 * row + x], z, y, x)
            store_operands(partner_rows(coords, alive), 3 * row + x, b_ref, x_ref)
            a_ref[row, :, N * x : N * (x + 1)] = own_rows(coords).astype(BF16)
            acc_out[3 * row + x] = jnp.zeros((16, N), F32)
            bond_out[3 * row + x] = bond_cell(
                own[3 * row + x], bonds[z, y, x, 0:1], bonds[z, y, x, 1:2], counts[z, y, x],
            )
        return 0

    lax.fori_loop(0, 9, prepare, 0)

    def sweep(step, _):
        z, other = z_pair(step)
        blocks = [
            (3 * z + y, x, 9 * other + 3 * near + x, y)
            for y in range(3)
            for near in range(max(0, y - 1), min(2, y + 1) + 1)
            for x in range(3)
        ]
        push_rows(acc_out, blocks, b_ref, x_ref, a_ref)
        return 0

    lax.fori_loop(0, 7, sweep, 0)


def bond_cell(cell, heads, tails, count):
    place = lax.broadcasted_iota(jnp.int32, (N, N), 0)
    pick = (place == tails).astype(F32) - (place == heads).astype(F32)
    pick = pick.astype(BF16)
    both = ((heads < count) & (tails < count)).astype(F32)
    zeros = jnp.zeros((4, N), F32)
    split = jnp.concatenate(list(three(cell)) + [zeros], axis=0).astype(BF16)
    found = product(split, pick)
    tension = both * (found[0:4] + found[4:8] + found[8:12])
    split = jnp.concatenate(list(three(tension)) + [zeros], axis=0).astype(BF16)
    back = product(split, pick, True)
    return -(back[0:4] + back[4:8] + back[8:12])


def other_pairs(middle, left, right, acc_in, acc, b_ref, x_ref, a_ref):
    def prepare(row, _):
        p, y = row // 5 - 1, row % 5 - 1
        for x in range(-1, 4):
            cell = left[row] if x == -1 else right[row] if x == 3 else middle[3 * row + x]
            coords, alive = scaled_cell(cell, p, y, x)
            store_operands(partner_rows(coords, alive), 5 * row + x + 1, b_ref, x_ref)
        return 0

    lax.fori_loop(0, 25, prepare, 0)

    def prepare_own(row, _):
        z, y = row // 3, row % 3
        for x in range(3):
            cell = middle[3 * (5 * (z + 1) + y + 1) + x]
            coords, alive = scaled_cell(cell, z, y, x)
            a_ref[row, :, N * x : N * (x + 1)] = own_rows(coords).astype(BF16)
            acc[3 * row + x] = acc_in[3 * row + x]
        return 0

    lax.fori_loop(0, 9, prepare_own, 0)

    def row_blocks(row, at_row, columns, tag):
        return [(row, x, 5 * at_row + x + 1, tag) for x in columns]

    def within(step, _):
        z, other = z_pair(step)
        blocks = []
        for y in range(3):
            for near in range(y - 1, y + 2):
                columns = (-1, 3) if 0 <= near <= 2 else range(-1, 4)
                blocks += row_blocks(3 * z + y, 5 * (other + 1) + near + 1, columns, y)
        push_rows(acc, blocks, b_ref, x_ref, a_ref)
        return 0

    lax.fori_loop(0, 7, within, 0)

    def across(step, _):
        side, y = step // 3, step % 3
        blocks = []
        for near in range(-1, 2):
            blocks += row_blocks(6 * side + y, 20 * side + y + near + 1, range(-1, 4), 0)
        push_rows(acc, blocks, b_ref, x_ref, a_ref)
        return 0

    lax.fori_loop(0, 6, across, 0)


def step_one(
    middle, left, right, acc_in, bond, vel, forces, own, top, bottom, acc, b_ref, x_ref, a_ref
):
    other_pairs(middle, left, right, acc_in, acc, b_ref, x_ref, a_ref)
    for z in range(3):
        for y in range(3):
            for x in range(3):
                at = 9 * z + 3 * y + x
                cell = middle[3 * (5 * (z + 1) + y + 1) + x]
                coords, _ = scaled_cell(cell, z, y, x)
                force = (cell_force(acc[at], coords) + bond[at][0:3]) * cell[3:4]
                speed = jnp.concatenate([vel[k, z, y, x : x + 1, :] for k in range(3)], axis=0)
                moved = cell[0:3] + STEP_DT * speed + 0.5 * STEP_DT * STEP_DT * force
                fresh = jnp.concatenate([moved, cell[3:4]], axis=0)
                own[at] = fresh
                if z == 2:
                    top[at - 18] = fresh
                if z == 0:
                    bottom[at] = fresh
                for k in range(3):
                    forces[k, z, y, x : x + 1, :] = force[k : k + 1]


def step_two(middle, left, right, acc_in, bond, carried, bottom, acc, b_ref, x_ref, a_ref):
    other_pairs(middle, left, right, acc_in, acc, b_ref, x_ref, a_ref)
    for z in range(3):
        for y in range(3):
            for x in range(3):
                at = 9 * z + 3 * y + x
                cell = middle[3 * (5 * (z + 1) + y + 1) + x]
                coords, _ = scaled_cell(cell, z, y, x)
                force = (cell_force(acc[at], coords) + bond[at][0:3]) * cell[3:4]
                both = jnp.concatenate([cell[0:3] * cell[3:4], force], axis=0)
                carried[at] = both
                if z < 2:
                    bottom[6 * at : 6 * at + 6] = both


HAND_CELLS = [
    (p, y, x) for p in range(5) for y in range(2 if p < 3 else 3) for x in range(3)
]
HAND_AT = {cell: at for at, cell in enumerate(HAND_CELLS)}


def rows6(ref, at):
    return ref[6 * at : 6 * at + 6]


def pack_hand(own, high, out):
    for (p, y, x), at in HAND_AT.items():
        value = own[9 * p + 3 * y + x] if p < 3 else rows6(high, 9 * (p - 3) + 3 * y + x)
        out[6 * at : 6 * at + 6] = value


def partner_six(high, swapped, p, y, x):
    there = rows6(swapped, HAND_AT[p, y, x])
    if p < 3:
        return there
    return jnp.where(highest_plane(), rows6(high, 9 * (p - 3) + 3 * y + x), there)


def pack_hand_relay(high, swapped, out):
    for p in range(5):
        for y in range(2):
            for x in range(3):
                at = 6 * p + 3 * y + x
                out[6 * at : 6 * at + 6] = partner_six(high, swapped, p, y, x)


def pack_hand_side(own, high, swapped, relayed, middle, side):
    even = even_column()
    for p in range(5):
        for y in range(5):
            for x in range(3):
                if y >= 3:
                    near = partner_six(high, swapped, p, y - 3, x)
                    far = rows6(relayed, 6 * p + 3 * (y - 3) + x)
                    value = jnp.where(even, near, far)
                elif p < 3:
                    value = own[9 * p + 3 * y + x]
                else:
                    near = rows6(high, 9 * (p - 3) + 3 * y + x)
                    far = rows6(swapped, HAND_AT[p, y, x])
                    value = jnp.where(highest_plane(), far, near)
                middle[15 * p + 3 * y + x] = value
                if x < 2:
                    at = 10 * p + 2 * y + x
                    side[6 * at : 6 * at + 6] = value


def place(plan_z, plan_y, plan_x, middle, side, moved, forces, ext):
    i, j, k = (lax.axis_index(name) for name in ("gz", "gy", "gx"))
    lows = (plan_z[(i + 15) % 16], plan_y[(j + 7) % 8, i], plan_x[j, (k + 7) % 8, i])
    fills = [
        3 + up - low for up, low in zip((plan_z[i], plan_y[j, i], plan_x[j, k, i]), lows)
    ]
    for row in range(25):
        for x in range(3):
            ext[5 * row + x, 0:6] = middle[3 * row + x]
        for x in range(2):
            ext[5 * row + 3 + x, 0:6] = rows6(side, 2 * row + x)

    def plane(s, _):
        z = jnp.minimum(lows[0] + s, 4)
        for t in range(5):
            y = jnp.minimum(lows[1] + t, 4)
            for u in range(5):
                x = jnp.minimum(lows[2] + u, 4)
                used = (s < fills[0]) & (t < fills[1]) & (u < fills[2])
                value = jnp.where(used, ext[25 * z + 5 * y + x], 0.0)
                moved[s, t, u] = value[0:3]
                forces[s, t, u] = value[3:6]
        return 0

    lax.fori_loop(0, 5, plane, 0)


def gz_gy(z, y):
    return (z % 16) * 8 + 2 * y + z // 16


def z_ring(block, distance):
    route = [
        (gz_gy((z - distance) % 32, y), gz_gy(z, y)) for z in range(32) for y in range(4)
    ]
    return lax.ppermute(block, ("gz", "gy"), route)


def swap(block):
    return lax.ppermute(block, "gy", [(i ^ 1, i) for i in range(8)])


def relay(block, up_to_odd_only=False):
    pairs = [((i - 2 if i % 2 == 0 else i + 2) % 8, i) for i in range(8)]
    if up_to_odd_only:
        pairs = [pair for pair in pairs if pair[1] % 2 == 1]
    return lax.ppermute(block, "gy", pairs)


def along_x(block, distance):
    return lax.ppermute(block, "gx", [((i - distance) % 8, i) for i in range(8)])


def halo_and_own(own, top, bottom, counts, bonds):
    low = z_ring(top, 1)
    high = z_ring(bottom, -1)
    (message,) = call(pack_swap, "pack_swap", (own, low, high), [(36, 4, N)])
    swapped = swap(message)
    acc, bond = call(
        own_pairs, "own_pairs", (own, counts, bonds), [(27, 16, N), (27, 4, N)],
        [pltpu.VMEM((27, N, 32), BF16), pltpu.VMEM((27, 16, N), BF16),
         pltpu.VMEM((9, 32, 3 * N), BF16)],
        [V, S, V],
    )
    (message,) = call(
        pack_relay, "pack_relay", (low, high, swapped), [(15, 4, N)]
    )
    relayed = relay(message)
    middle, left, right = call(
        pack_middle, "pack_middle", (own, low, high, swapped, relayed),
        [(75, 4, N), (25, 4, N), (25, 4, N)],
    )
    return middle, along_x(right, 1), along_x(left, -1), acc, bond


PAIR_SCRATCH = [
    pltpu.VMEM((27, 16, N), F32), pltpu.VMEM((125, N, 32), BF16),
    pltpu.VMEM((125, 16, N), BF16), pltpu.VMEM((9, 32, 3 * N), BF16),
]


def on_device(positions, velocities, counts, bonds, plan_z, plan_y, plan_x):
    bonds = jnp.moveaxis(bonds, 0, 3)
    own, top, bottom = call(
        pack_first, "pack_first", (positions, counts), [(27, 4, N), (9, 4, N), (9, 4, N)], (),
        [V, S],
    )
    middle, left, right, acc, bond = halo_and_own(own, top, bottom, counts, bonds)
    forces_first, own, top, bottom = call(
        step_one, "step_one", (middle, left, right, acc, bond, velocities),
        [(3, 3, 3, 3, N), (27, 4, N), (9, 4, N), (9, 4, N)], PAIR_SCRATCH,
    )
    middle, left, right, acc, bond = halo_and_own(own, top, bottom, counts, bonds)
    own, bottom = call(
        step_two, "step_two", (middle, left, right, acc, bond), [(27, 6, N), (108, N)],
        PAIR_SCRATCH,
    )
    high = z_ring(bottom, -1)
    (message,) = call(pack_hand, "pack_hand", (own, high), [(216, N)])
    swapped = swap(message)
    (message,) = call(
        pack_hand_relay, "pack_hand_relay", (high, swapped), [(180, N)]
    )
    relayed = relay(message, True)
    middle, side = call(
        pack_hand_side, "pack_hand_side", (own, high, swapped, relayed),
        [(75, 6, N), (300, N)],
    )
    side = along_x(side, -1)
    moved_positions, moved_forces = call(
        place, "place", (plan_z, plan_y.T, plan_x.transpose(1, 2, 0), middle, side),
        [(5, 5, 5, 3, N), (5, 5, 5, 3, N)], [pltpu.VMEM((125, 8, N), F32)], [S, S, S, V, V],
        to_hbm=True,
    )
    return forces_first, jnp.moveaxis(moved_positions, 3, 0), jnp.moveaxis(moved_forces, 3, 0)


def solution(mesh):
    bricks = P(None, "gz", "gy", "gx", None)
    return jax.shard_map(
        on_device,
        mesh=mesh,
        in_specs=(bricks, bricks, P("gz", "gy", "gx"), bricks, P(), P(), P()),
        out_specs=(bricks, bricks, bricks),
        check_vma=False,
    )
```

```python
import functools
import math

import jax
import jax.numpy as jnp
from jax import lax
from jax.experimental import pallas as pl
from jax.experimental.pallas import tpu as pltpu
from jax.sharding import PartitionSpec as P

STRENGTH = 0.3
SPREAD = 0.6
STEP_DT = 0.2
F32 = jnp.float32
BF16 = jnp.bfloat16
SCALE = math.sqrt(1.0 / (SPREAD * math.log(2.0)))
PUSH = STRENGTH / SCALE
DEAD = -1.0e6
N = 128
V = pl.BlockSpec(memory_space=pltpu.VMEM)
S = pl.BlockSpec(memory_space=pltpu.SMEM)


def call(kernel, name, ins, outs, scratch=(), specs=None, to_hbm=False):
    specs = [V] * len(ins) if specs is None else specs
    return pl.pallas_call(
        kernel,
        name=name,
        out_shape=[
            jax.ShapeDtypeStruct(shape, F32) if to_hbm
            else pltpu.VMEM(shape, F32) if isinstance(shape, tuple) else shape
            for shape in outs
        ],
        in_specs=specs,
        out_specs=[V] * len(outs),
        scratch_shapes=list(scratch),
    )(*[
        pltpu.with_memory_space_constraint(value, pltpu.VMEM) if spec is V else value
        for value, spec in zip(ins, specs)
    ])


def living_row(count):
    return (lax.broadcasted_iota(jnp.int32, (1, N), 1) < count).astype(F32)


def pack_first(pos, counts, own, top, bottom):
    for z in range(3):
        for y in range(3):
            for x in range(3):
                rows = [pos[k, z, y, x : x + 1, :] for k in range(3)]
                cell = jnp.concatenate(rows + [living_row(counts[z, y, x])], axis=0)
                own[9 * z + 3 * y + x] = cell
                if z == 2:
                    top[3 * y + x] = cell
                if z == 0:
                    bottom[3 * y + x] = cell


SWAP_CELLS = [
    (p, y, x)
    for p in range(-1, 4)
    for y in (range(3) if p in (-1, 3) else (0, 2))
    for x in range(3)
]
SWAP_AT = {cell: at for at, cell in enumerate(SWAP_CELLS)}


def pack_swap(own, low, high, out):
    for (p, y, x), at in SWAP_AT.items():
        if p == -1:
            out[at] = low[3 * y + x]
        elif p == 3:
            out[at] = high[3 * y + x]
        else:
            out[at] = own[9 * p + 3 * y + x]


def even_column():
    return lax.axis_index("gy") % 2 == 0


def lowest_plane():
    return lax.axis_index("gz") == 0


def highest_plane():
    return lax.axis_index("gz") == 15


def partner_cell(low, high, swapped, p, y, x):
    there = swapped[SWAP_AT[p, y, x]]
    if p == -1:
        return jnp.where(lowest_plane(), low[3 * y + x], there)
    if p == 3:
        return jnp.where(highest_plane(), high[3 * y + x], there)
    return there


def own_cell(own, low, high, swapped, p, y, x):
    if p == -1:
        return jnp.where(lowest_plane(), swapped[SWAP_AT[p, y, x]], low[3 * y + x])
    if p == 3:
        return jnp.where(highest_plane(), swapped[SWAP_AT[p, y, x]], high[3 * y + x])
    return own[9 * p + 3 * y + x]


def pack_relay(low, high, swapped, out):
    even = even_column()
    for p in range(-1, 4):
        for x in range(3):
            upper = partner_cell(low, high, swapped, p, 2, x)
            lower = partner_cell(low, high, swapped, p, 0, x)
            out[3 * (p + 1) + x] = jnp.where(even, upper, lower)


def pack_middle(own, low, high, swapped, relayed, middle, left, right):
    even = even_column()
    for p in range(-1, 4):
        for y in range(-1, 4):
            for x in range(3):
                if y in (-1, 3):
                    near = partner_cell(low, high, swapped, p, 2 if y == -1 else 0, x)
                    far = relayed[3 * (p + 1) + x]
                    if y == -1:
                        near, far = far, near
                    cell = jnp.where(even, near, far)
                else:
                    cell = own_cell(own, low, high, swapped, p, y, x)
                row = 5 * (p + 1) + y + 1
                middle[3 * row + x] = cell
                if x == 0:
                    left[row] = cell
                if x == 2:
                    right[row] = cell


def three(x):
    first = x.astype(BF16).astype(F32)
    rest = x - first
    second = rest.astype(BF16).astype(F32)
    return first, second, rest - second


def scaled_cell(cell, p, y, x):
    alive = cell[3:4] > 0.5
    at = lax.broadcasted_iota(jnp.int32, (3, 1), 0)
    shift = jnp.where(at == 0, p, jnp.where(at == 1, y, x)).astype(F32) - 1.5
    return jnp.where(alive, (cell[0:3] + shift) * SCALE, 0.0), alive


def partner_rows(coords, alive):
    norm = jnp.where(alive, -jnp.sum(coords * coords, axis=0, keepdims=True), DEAD)
    b1, b2, b3 = three(jnp.concatenate([coords, norm], axis=0))
    ones = jnp.concatenate([jnp.ones((3, N), F32), jnp.zeros((1, N), F32)], axis=0)
    zeros = jnp.zeros((4, N), F32)
    return jnp.concatenate([zeros, b1, b1, b2, b1, b2, b3, ones], axis=0)


def own_rows(coords):
    norm = -jnp.sum(coords * coords, axis=0, keepdims=True)
    a1, a2, a3 = three(jnp.concatenate([2.0 * coords, jnp.ones((1, N), F32)], axis=0))
    zeros = jnp.zeros((1, N), F32)
    tail = jnp.concatenate(list(three(norm)) + [zeros], axis=0)
    return jnp.concatenate([jnp.zeros((4, N), F32), a1, a2, a1, a3, a2, a1, tail], axis=0)


def product(left, right, right_turned=False):
    dims = (((1,), (1 if right_turned else 0,)), ((), ()))
    return lax.dot_general(left, right, dims, preferred_element_type=F32)


def store_operands(rows, at, b_ref, x_ref):
    b_ref[at] = rows.T.astype(BF16)
    x_ref[at] = rows[16:32].astype(BF16)


AHEAD = 12
OWN_CUTS = (2, 5)


def push_rows(acc_ref, blocks, b_ref, x_ref, a_ref):
    def reach(block):
        return max(0, block[1] - 1), min(2, block[1] + 1) + 1

    def exponents(block):
        first, last = reach(block)
        return product(b_ref[block[2]], a_ref[block[0], :, N * first : N * last])

    waiting = [exponents(block) for block in blocks[:AHEAD]]
    sums = [None, None, None]
    for at, block in enumerate(blocks):
        if at + AHEAD < len(blocks):
            waiting.append(exponents(blocks[at + AHEAD]))
        weight = jnp.exp2(waiting.pop(0))
        high = weight.astype(BF16)
        low = (weight - high.astype(F32)).astype(BF16)
        x_op = x_ref[block[2]]
        value = product(
            jnp.concatenate([x_op, x_op], axis=1), jnp.concatenate([high, low], axis=0)
        )
        first, last = reach(block)
        for x in range(first, last):
            part = value[:, N * (x - first) : N * (x - first + 1)]
            sums[x] = part if sums[x] is None else sums[x] + part
        if at + 1 == len(blocks) or blocks[at + 1][3] != block[3]:
            for x in range(3):
                if sums[x] is not None:
                    acc_ref[3 * block[0] + x] += sums[x]
            sums = [None, None, None]


def cell_force(acc, coords):
    total = acc[0:4] + acc[4:8] + acc[8:12]
    return PUSH * (coords * acc[12:15] - total[0:3])


def z_pair(step):
    z = (step + 1) // 3
    return z, step - 2 * z


def each(count, group, body):
    def several(start, _):
        for step in range(group):
            body(group * start + step, 0)
        return 0

    lax.fori_loop(0, count // group, several, 0)


def own_sweeps(first, last, acc, b_ref, x_ref, a_ref):
    def sweep(step, _):
        z, other = z_pair(step)
        blocks = [
            (3 * z + y, x, 9 * other + 3 * near + x, y)
            for y in range(3)
            for near in range(max(0, y - 1), min(2, y + 1) + 1)
            for x in range(3)
        ]
        push_rows(acc, blocks, b_ref, x_ref, a_ref)
        return 0

    lax.fori_loop(first, last, sweep, 0)


def own_start(own, counts, bonds, acc, bond_out, b_ref, x_ref, a_ref):
    def prepare(row, _):
        z, y = row // 3, row % 3
        for x in range(3):
            coords, alive = scaled_cell(own[3 * row + x], z, y, x)
            store_operands(partner_rows(coords, alive), 3 * row + x, b_ref, x_ref)
            a_ref[row, :, N * x : N * (x + 1)] = own_rows(coords).astype(BF16)
            acc[3 * row + x] = jnp.zeros((16, N), F32)
            bond_out[3 * row + x] = bond_cell(
                own[3 * row + x], bonds[z, y, x, 0:1], bonds[z, y, x, 1:2], counts[z, y, x]
            )
        return 0

    each(9, 3, prepare)
    own_sweeps(0, OWN_CUTS[0], acc, b_ref, x_ref, a_ref)


def own_more(acc_in, b_ref, x_ref, a_ref, acc, *, first, last):
    acc[...] = acc_in[...]
    own_sweeps(first, last, acc, b_ref, x_ref, a_ref)


def bond_cell(cell, heads, tails, count):
    place = lax.broadcasted_iota(jnp.int32, (N, N), 0)
    pick = (place == tails).astype(F32) - (place == heads).astype(F32)
    pick = pick.astype(BF16)
    both = ((heads < count) & (tails < count)).astype(F32)
    zeros = jnp.zeros((4, N), F32)
    split = jnp.concatenate(list(three(cell)) + [zeros], axis=0).astype(BF16)
    found = product(split, pick)
    tension = both * (found[0:4] + found[4:8] + found[8:12])
    split = jnp.concatenate(list(three(tension)) + [zeros], axis=0).astype(BF16)
    back = product(split, pick, True)
    return -(back[0:4] + back[4:8] + back[8:12])


def other_pairs(middle, left, right, acc_in, a_ref, acc, b_ref, x_ref):
    acc[...] = acc_in[...]

    def prepare(cell, row, x):
        coords, alive = scaled_cell(cell, row // 5 - 1, row % 5 - 1, x)
        store_operands(partner_rows(coords, alive), 5 * row + x + 1, b_ref, x_ref)

    def prepare_sides(row, _):
        prepare(left[row], row, -1)
        prepare(right[row], row, 3)
        return 0

    each(25, 5, prepare_sides)

    def prepare_around(step, _):
        inner = step - 10
        row = jnp.where(step < 5, step, jnp.where(step < 10, step + 15, 0))
        row = jnp.where(step < 10, row, 5 * (1 + inner // 2) + 4 * (inner % 2))
        for x in range(3):
            prepare(middle[3 * row + x], row, x)
        return 0

    each(16, 4, prepare_around)

    def row_blocks(row, at_row, columns, tag):
        return [(row, x, 5 * at_row + x + 1, tag) for x in columns]

    def within(step, _):
        z, other = z_pair(step)
        blocks = []
        for y in range(3):
            for near in range(y - 1, y + 2):
                columns = (-1, 3) if 0 <= near <= 2 else range(-1, 4)
                blocks += row_blocks(3 * z + y, 5 * (other + 1) + near + 1, columns, y)
        push_rows(acc, blocks, b_ref, x_ref, a_ref)
        return 0

    lax.fori_loop(0, 7, within, 0)

    def across(step, _):
        side, y = step // 3, step % 3
        blocks = []
        for near in range(-1, 2):
            blocks += row_blocks(6 * side + y, 20 * side + y + near + 1, range(-1, 4), 0)
        push_rows(acc, blocks, b_ref, x_ref, a_ref)
        return 0

    lax.fori_loop(0, 6, across, 0)


def step_one(
    middle, left, right, acc_in, bond, a_ref, vel, forces, own, top, bottom, acc, b_ref, x_ref
):
    other_pairs(middle, left, right, acc_in, a_ref, acc, b_ref, x_ref)
    for z in range(3):
        for y in range(3):
            for x in range(3):
                at = 9 * z + 3 * y + x
                cell = middle[3 * (5 * (z + 1) + y + 1) + x]
                coords, _ = scaled_cell(cell, z, y, x)
                force = (cell_force(acc[at], coords) + bond[at][0:3]) * cell[3:4]
                speed = jnp.concatenate([vel[k, z, y, x : x + 1, :] for k in range(3)], axis=0)
                moved = cell[0:3] + STEP_DT * speed + 0.5 * STEP_DT * STEP_DT * force
                fresh = jnp.concatenate([moved, cell[3:4]], axis=0)
                own[at] = fresh
                if z == 2:
                    top[at - 18] = fresh
                if z == 0:
                    bottom[at] = fresh
                for k in range(3):
                    forces[k, z, y, x : x + 1, :] = force[k : k + 1]


def step_two(middle, left, right, acc_in, bond, a_ref, carried, message, acc, b_ref, x_ref):
    other_pairs(middle, left, right, acc_in, a_ref, acc, b_ref, x_ref)
    for z in range(3):
        for y in range(3):
            for x in range(3):
                at = 9 * z + 3 * y + x
                cell = middle[3 * (5 * (z + 1) + y + 1) + x]
                coords, _ = scaled_cell(cell, z, y, x)
                force = (cell_force(acc[at], coords) + bond[at][0:3]) * cell[3:4]
                both = jnp.concatenate([cell[0:3] * cell[3:4], force], axis=0)
                carried[at] = both
                if (z, y, x) in HAND_AT:
                    to = HAND_AT[z, y, x]
                    message[6 * to : 6 * to + 6] = both


HAND_CELLS = [
    (p, y, x) for p in range(3) for y in range(3 if p < 2 else 2) for x in range(3)
]
HAND_AT = {cell: at for at, cell in enumerate(HAND_CELLS)}


def rows6(ref, at):
    return ref[6 * at : 6 * at + 6]


def pack_up(own, swapped, out):
    for p in range(2):
        for y in range(3):
            for x in range(3):
                at = 9 * p + 3 * y + x
                out[6 * at : 6 * at + 6] = own[at]
                out[6 * (18 + at) : 6 * (18 + at) + 6] = rows6(swapped, HAND_AT[p, y, x])


def above(upper, p, y, x, partner):
    at = 9 * (p - 3) + 3 * y + x
    same, crossed = rows6(upper, at), rows6(upper, 18 + at)
    if partner:
        same, crossed = crossed, same
    return jnp.where(highest_plane(), crossed, same)


def partner_six(swapped, upper, p, y, x):
    return rows6(swapped, HAND_AT[p, y, x]) if p < 3 else above(upper, p, y, x, True)


def pack_hand_relay(swapped, upper, out):
    for p in range(5):
        for y in range(2):
            for x in range(3):
                at = 6 * p + 3 * y + x
                out[6 * at : 6 * at + 6] = partner_six(swapped, upper, p, y, x)


def pack_hand_side(own, swapped, upper, relayed, middle, side):
    even = even_column()
    for p in range(5):
        for y in range(5):
            for x in range(3):
                if y >= 3:
                    near = partner_six(swapped, upper, p, y - 3, x)
                    far = rows6(relayed, 6 * p + 3 * (y - 3) + x)
                    value = jnp.where(even, near, far)
                elif p < 3:
                    value = own[9 * p + 3 * y + x]
                else:
                    value = above(upper, p, y, x, False)
                middle[15 * p + 3 * y + x] = value
                if x < 2:
                    at = 10 * p + 2 * y + x
                    side[6 * at : 6 * at + 6] = value


def place(plan_z, plan_y, plan_x, middle, side, moved, forces, ext):
    i, j, k = (lax.axis_index(name) for name in ("gz", "gy", "gx"))
    lows = (plan_z[(i + 15) % 16], plan_y[(j + 7) % 8, i], plan_x[j, (k + 7) % 8, i])
    fills = [
        3 + up - low for up, low in zip((plan_z[i], plan_y[j, i], plan_x[j, k, i]), lows)
    ]
    for row in range(25):
        for x in range(3):
            ext[5 * row + x, 0:6] = middle[3 * row + x]
        for x in range(2):
            ext[5 * row + 3 + x, 0:6] = rows6(side, 2 * row + x)

    def plane(s, _):
        z = jnp.minimum(lows[0] + s, 4)
        for t in range(5):
            y = jnp.minimum(lows[1] + t, 4)
            for u in range(5):
                x = jnp.minimum(lows[2] + u, 4)
                used = (s < fills[0]) & (t < fills[1]) & (u < fills[2])
                value = jnp.where(used, ext[25 * z + 5 * y + x], 0.0)
                moved[s, t, u] = value[0:3]
                forces[s, t, u] = value[3:6]
        return 0

    lax.fori_loop(0, 5, plane, 0)


def gz_gy(z, y):
    return (z % 16) * 8 + 2 * y + z // 16


def z_ring(block, distance):
    route = [
        (gz_gy((z - distance) % 32, y), gz_gy(z, y)) for z in range(32) for y in range(4)
    ]
    return lax.ppermute(block, ("gz", "gy"), route)


def swap(block):
    return lax.ppermute(block, "gy", [(i ^ 1, i) for i in range(8)])


def relay(block, up_to_odd_only=False):
    pairs = [((i - 2 if i % 2 == 0 else i + 2) % 8, i) for i in range(8)]
    if up_to_odd_only:
        pairs = [pair for pair in pairs if pair[1] % 2 == 1]
    return lax.ppermute(block, "gy", pairs)


def along_x(block, distance):
    return lax.ppermute(block, "gx", [((i - distance) % 8, i) for i in range(8)])


def halo_and_own(own, top, bottom, counts, bonds):
    low = z_ring(top, 1)
    high = z_ring(bottom, -1)
    (message,) = call(pack_swap, "pack_swap", (own, low, high), [(36, 4, N)])
    swapped = swap(message)
    acc, bond, *operands = call(
        own_start, "own_start", (own, counts, bonds),
        [(27, 16, N), (27, 4, N), pltpu.VMEM((27, N, 32), BF16),
         pltpu.VMEM((27, 16, N), BF16), pltpu.VMEM((9, 32, 3 * N), BF16)],
        (), [V, S, V],
    )
    (message,) = call(
        after(pack_relay), "pack_relay", (acc, low, high, swapped), [(15, 4, N)]
    )
    relayed = relay(message)
    for part in range(2):
        if part == 1:
            middle, left, right = call(
                after(pack_middle), "pack_middle", (acc, own, low, high, swapped, relayed),
                [(75, 4, N), (25, 4, N), (25, 4, N)],
            )
        cuts = OWN_CUTS + (7,)
        (acc,) = call(
            functools.partial(own_more, first=cuts[part], last=cuts[part + 1]),
            f"own_more_{part}", (acc, *operands), [(27, 16, N)],
        )
    return middle, along_x(right, 1), along_x(left, -1), acc, bond, operands[2]


def after(kernel):
    return lambda waited, *refs: kernel(*refs)


PAIR_SCRATCH = [
    pltpu.VMEM((27, 16, N), F32), pltpu.VMEM((125, N, 32), BF16),
    pltpu.VMEM((125, 16, N), BF16),
]


def on_device(positions, velocities, counts, bonds, plan_z, plan_y, plan_x):
    bonds = jnp.moveaxis(bonds, 0, 3)
    own, top, bottom = call(
        pack_first, "pack_first", (positions, counts), [(27, 4, N), (9, 4, N), (9, 4, N)], (),
        [V, S],
    )
    halo = halo_and_own(own, top, bottom, counts, bonds)
    forces_first, own, top, bottom = call(
        step_one, "step_one", (*halo, velocities),
        [(3, 3, 3, 3, N), (27, 4, N), (9, 4, N), (9, 4, N)], PAIR_SCRATCH,
    )
    halo = halo_and_own(own, top, bottom, counts, bonds)
    own, message = call(step_two, "step_two", halo, [(27, 6, N), (144, N)], PAIR_SCRATCH)
    swapped = swap(message)
    (message,) = call(pack_up, "pack_up", (own, swapped), [(216, N)])
    upper = z_ring(message, -1)
    (message,) = call(pack_hand_relay, "pack_hand_relay", (swapped, upper), [(180, N)])
    relayed = relay(message, True)
    middle, side = call(
        pack_hand_side, "pack_hand_side", (own, swapped, upper, relayed),
        [(75, 6, N), (300, N)],
    )
    side = along_x(side, -1)
    moved_positions, moved_forces = call(
        place, "place", (plan_z, plan_y.T, plan_x.transpose(1, 2, 0), middle, side),
        [(5, 5, 5, 3, N), (5, 5, 5, 3, N)], [pltpu.VMEM((125, 8, N), F32)], [S, S, S, V, V],
        to_hbm=True,
    )
    return forces_first, jnp.moveaxis(moved_positions, 3, 0), jnp.moveaxis(moved_forces, 3, 0)


def solution(mesh):
    bricks = P(None, "gz", "gy", "gx", None)
    return jax.shard_map(
        on_device,
        mesh=mesh,
        in_specs=(bricks, bricks, P("gz", "gy", "gx"), bricks, P(), P(), P()),
        out_specs=(bricks, bricks, bricks),
        check_vma=False,
    )
```
